512 devices in a mesh: seq: 16 (over x, y), tensor: 32 (over z, core).
Axes of the slice: x: 4, y: 4, z: 16, core: 2. Of those that a mesh axis runs over, the one named last changes fastest.
Arguments:
- hidden: bfloat16 [256, 2048], P('seq', 'tensor'), may hold values from -6 to 6
- router_logits: float32 [256, 8], replicated, may hold values from -6 to 6
- routes: int32 [256, 2], replicated, may hold values from 0 to 7, all different within a row
- w_query: bfloat16 [8, 2048, 2048], P(None, 'tensor', 'seq'), may hold values from -0.125 to 0.125
- w_keyval: bfloat16 [2048, 2, 2048], P('tensor', None, 'seq'), may hold values from -0.125 to 0.125
- w_output: bfloat16 [8, 2048, 2048], P(None, 'seq', 'tensor'), may hold values from -0.125 to 0.125
- k_cache: bfloat16 [4096, 64, 2048], P(('seq', 'tensor')), may hold values from -720 to 720
- v_cache: bfloat16 [4096, 64, 2048], P(('seq', 'tensor')), may hold values from -6 to 6
- lengths: int32 [64], replicated, may hold values from 1 to 4096, 104857 in all
- page_table: int32 [64, 64], replicated, may hold values from 0 to 7, as said below
- home_device: int32 [64], replicated, may hold values from 0 to 15
- accepted: int32 [64], replicated, may hold values from 1 to 4
Outputs:
- attn_out: float32 [256, 2048], P('seq', 'tensor')
- new_keys: float32 [256, 2048], P('tensor', 'seq')
- new_values: float32 [256, 2048], P('tensor', 'seq')
The draws below stay inside these ranges and needn't reach their ends.
Inputs may be any that keep to these rules, and one draw needn't show every extreme that they name: `page_table`: for each index s of seq and t of tensor, the pages j of the requests r with r // 2 = t and (home_device[r] + j) % 16 = s have distinct values.
All inputs are finite; a program needn't handle non-finite values.
Results may differ from the reference program's by a relative error of at most 0.019.
Values may be sent and summed in bfloat16 or wider, within the bound.
A program may use at most 64 MiB of HBM per device.

```python
import math
import jax
import jax.numpy as jnp
import numpy as np
from jax import lax

D = 2048
E = 8
KVH = 16
HD = 128
Q = 4
PAGE = 64
MAXLEN = 4096
REQ_DEV = 2
REQ = 64
TOK = 256
MAXP = 64
PAGES_DEV = 4
SLOTS_DEV = 8
SLOTS = 4096
N_SEQ = 16
N_TENSOR = 32


def placement_helper(key):
    seq_devs = MAXP // PAGES_DEV
    tensor_devs = REQ // REQ_DEV
    shuffled = jax.random.permutation(jax.random.fold_in(key, 11), REQ)
    home_dev = (shuffled % seq_devs).astype(jnp.int32)
    slot_keys = jax.random.split(jax.random.fold_in(key, 23), tensor_devs * seq_devs)
    slot_orders = jax.vmap(lambda subkey: jax.random.permutation(subkey, SLOTS_DEV))(slot_keys)
    request_ids = jnp.arange(REQ, dtype=jnp.int32)[:, None]
    page_ids = jnp.arange(MAXP, dtype=jnp.int32)[None, :]
    seq_dev = (home_dev[:, None] + page_ids) % seq_devs
    tensor_dev = request_ids // REQ_DEV
    local_slot = request_ids % REQ_DEV * PAGES_DEV + page_ids // seq_devs
    slot_table = slot_orders[tensor_dev * seq_devs + seq_dev, local_slot]
    return (home_dev, slot_table.astype(jnp.int32))


def draw_home_device(key, part):
    return placement_helper(key)[0]


def draw_page_table(key, part):
    return placement_helper(key)[1]


def draw_k_cache(key, part):
    base_draw = jnp.clip(jax.random.normal(key, (SLOTS, PAGE, KVH * HD), jnp.float32), -6.0, 6.0)
    return base_draw.astype(jnp.bfloat16)


def with_ends(values, own_key, least, largest):
    index_at = [jax.random.randint(jax.random.fold_in(own_key, axis), (), 0, length) for axis, length in enumerate(values.shape)]
    main_axis = values.shape.index(max(values.shape))
    neighbour = index_at[:main_axis] + [(index_at[main_axis] + 1) % values.shape[main_axis]] + index_at[main_axis + 1:]
    return values.at[tuple(index_at)].set(least).at[tuple(neighbour)].set(largest)


def block_levels(stream_key, dims, shards, least, high):
    def one(position, parts):
        steps = jax.random.uniform(jax.random.fold_in(jax.random.fold_in(stream_key, 6), position), (parts,), jnp.float32, least / len(shards), high / len(shards))
        return jnp.repeat(jnp.exp(steps), dims[position] // parts).reshape((-1,) + (1,) * (len(dims) - position - 1))

    loudness = one(*shards[0])
    for cut in shards[1:]:
        loudness = loudness * one(*cut)
    return loudness


def picks_of(own_key, rows, amount, top, lift):
    order = jax.random.permutation(jax.random.fold_in(own_key, 1), amount)
    pull = order
    for power in range(3):
        pull = pull * pull // amount
    pull = pull * lift // amount
    lots = jax.random.randint(jax.random.fold_in(own_key, 2), (rows, amount), 0, 4096) + pull
    holders = jax.random.permutation(jax.random.fold_in(own_key, 3), rows)[jnp.arange(amount) % rows]
    lots = jnp.where(jnp.arange(rows)[:, None] == holders[None, :], 1 << 14, lots)
    merit = lots * amount + jnp.arange(amount)
    return lax.top_k(merit.astype(jnp.int32), top)[1].astype(jnp.int32)


def profile(number_of, total, most, slope):
    portions = [(1 << 20) // math.isqrt(standing ** slope) + 1 for standing in range(2, number_of + 1)]
    surplus, holding = total - most - (number_of - 1), [1] * (number_of - 1)
    while surplus > 0:
        free = [i for i in range(number_of - 1) if holding[i] < most]
        mass, left = sum([portions[i] for i in free]), surplus
        for i in free:
            addition = min(most - holding[i], max(1, left * portions[i] // mass), surplus)
            holding[i] = holding[i] + addition
            surplus = surplus - addition
    return np.array([most] + holding)


def uneven_parts(own_key, count, total, reach, lean):
    if count == 2:
        one = jax.random.randint(own_key, (), max(1, total - reach), min(reach, total - 1) + 1)
        return jnp.stack([one, total - one])
    sizes = jnp.asarray(profile(count, total, reach, lean), jnp.int32)
    pairs = (count - 1) // 2
    source_of, taker = sizes[1:1 + 2 * pairs:2], sizes[2:2 + 2 * pairs:2]
    margin = jnp.minimum(source_of - 1, reach - taker)
    shifted = jax.random.randint(jax.random.fold_in(own_key, 1), (pairs,), 0, 1 << 20) % (margin + 1)
    sizes = sizes.at[1:1 + 2 * pairs:2].set(source_of - shifted).at[2:2 + 2 * pairs:2].set(taker + shifted)
    return sizes[jax.random.permutation(jax.random.fold_in(own_key, 2), count)]


def noise(own_key, dims, spread, limit, cuts=(), held_as=jnp.bfloat16):
    level = block_levels(own_key, dims, cuts, -0.22, 0.18) if cuts else 1.0
    result = jax.random.normal(own_key, dims, jnp.float32) * spread * level
    return jnp.minimum(jnp.maximum(result, -limit), limit).astype(held_as)


def setup_inputs(seed: int = 0) -> dict:
    streams_of = jax.random.split(jax.random.key(seed), 13)
    hidden = noise(streams_of[0], (TOK, D), 1.0, 6.0, ((0, 16), (1, 32)))
    router_logits = noise(streams_of[1], (TOK, E), 1.5, 6.0, (), jnp.float32)
    routes = picks_of(streams_of[2], TOK, E, 2, 2048)
    w_query = noise(streams_of[3], (E, D, KVH * HD), D ** -0.5, 0.125, ((1, 32), (2, 16)))
    w_keyval = noise(streams_of[4], (D, 2, KVH * HD), D ** -0.5, 0.125, ((0, 32), (2, 16)))
    w_output = noise(streams_of[5], (E, KVH * HD, D), (KVH * HD) ** -0.5, 0.125, ((1, 16), (2, 32)))
    k_cache = draw_k_cache(jax.random.fold_in(streams_of[12], 71), 0)
    v_cache = noise(streams_of[7], (SLOTS, PAGE, KVH * HD), 1.0, 6.0, ((0, 512),))
    lengths = uneven_parts(streams_of[8], REQ, REQ * MAXLEN * 2 // 5, MAXLEN, 2).astype(jnp.int32)
    page_table = draw_page_table(jax.random.fold_in(streams_of[12], 71), 0)
    home_device = draw_home_device(jax.random.fold_in(streams_of[12], 71), 0)
    accepted = with_ends(jax.random.randint(streams_of[11], (REQ,), 1, Q + 1), jax.random.fold_in(streams_of[11], 1), 1, Q).astype(jnp.int32)
    return dict(hidden=hidden, router_logits=router_logits, routes=routes, w_query=w_query, w_keyval=w_keyval, w_output=w_output, k_cache=k_cache, v_cache=v_cache, lengths=lengths, page_table=page_table, home_device=home_device, accepted=accepted)


THETA = 10000.0

def rotate(vectors, positions):
    half_width = HD // 2
    inverse = THETA ** (-(jnp.arange(half_width, dtype=jnp.float32) * 2.0 / HD))
    angles = positions.astype(jnp.float32)[..., None] * inverse
    cosine = jnp.cos(angles)
    sine_vals = jnp.sin(angles)
    front_half = vectors[..., :half_width]
    back_half = vectors[..., half_width:]
    return jnp.concatenate([front_half * cosine - back_half * sine_vals, back_half * cosine + front_half * sine_vals], axis=-1)

def reference(hidden, router_logits, routes, w_query, w_keyval, w_output, k_cache, v_cache, lengths, page_table, home_device, accepted):
    tokens = hidden.shape[0]
    selector = routes[:, :, None] == jnp.arange(E, dtype=jnp.int32)[None, None, :]
    hidden_wide = hidden.astype(jnp.float32)
    query_every = jnp.einsum('nd,edh->neh', hidden_wide, w_query.astype(jnp.float32))
    query_two = lax.optimization_barrier(jnp.sum(jnp.where(selector[:, :, :, None], query_every[:, None, :, :], 0.0), axis=2))
    keyval = jnp.einsum('nd,dch->nch', hidden_wide, w_keyval.astype(jnp.float32))
    request_of = jnp.arange(tokens, dtype=jnp.int32) // Q
    step_of = jnp.arange(tokens, dtype=jnp.int32) % Q
    positions = lengths[request_of] + step_of
    queries = rotate(query_two.reshape(tokens, 2, KVH, HD), positions[:, None, None]).astype(jnp.bfloat16)
    keys_rotated = rotate(keyval[:, 0].reshape(tokens, KVH, HD), positions[:, None])
    values_raw = keyval[:, 1].reshape(tokens, KVH, HD)
    keys_fresh = keys_rotated.astype(jnp.bfloat16)
    values_fresh = values_raw.astype(jnp.bfloat16)
    queries = lax.optimization_barrier(queries)
    keys_fresh = lax.optimization_barrier(keys_fresh)
    values_fresh = lax.optimization_barrier(values_fresh)
    scaling = 1.0 / math.sqrt(HD)
    key_slots = jnp.arange(MAXP * PAGE, dtype=jnp.int32)
    causal = jnp.arange(Q, dtype=jnp.int32)[:, None] >= jnp.arange(Q, dtype=jnp.int32)[None, :]

    def one_request(request):
        page_ids = jnp.arange(MAXP, dtype=jnp.int32)
        seq_dev = (home_device[request] + page_ids) % N_SEQ
        tensor_dev = request // REQ_DEV
        global_slot = ((seq_dev * N_TENSOR + tensor_dev) * SLOTS_DEV + page_table[request]).astype(jnp.int32)
        cache_keys = k_cache[global_slot].reshape(MAXP * PAGE, KVH, HD).astype(jnp.float32)
        cache_values = v_cache[global_slot].reshape(MAXP * PAGE, KVH, HD).astype(jnp.float32)
        first_row = (request * Q).astype(jnp.int32)
        own_queries = lax.dynamic_slice_in_dim(queries, first_row, Q, 0).astype(jnp.float32)
        own_keys = lax.dynamic_slice_in_dim(keys_fresh, first_row, Q, 0).astype(jnp.float32)
        own_values = lax.dynamic_slice_in_dim(values_fresh, first_row, Q, 0).astype(jnp.float32)
        old_scores = jnp.einsum('qkhd,thd->qkht', own_queries, cache_keys) * scaling
        old_valid = key_slots < lengths[request]
        old_scores = jnp.where(old_valid[None, None, None, :], old_scores, -jnp.inf)
        new_scores = jnp.einsum('qkhd,thd->qkht', own_queries, own_keys) * scaling
        new_scores = jnp.where(causal[:, None, None, :], new_scores, -jnp.inf)
        top_score = jnp.maximum(lax.optimization_barrier(jnp.max(old_scores, axis=-1)), lax.optimization_barrier(jnp.max(new_scores, axis=-1)))
        old_weights = jnp.exp(old_scores - top_score[..., None])
        new_weights = jnp.exp(new_scores - top_score[..., None])
        totals = lax.optimization_barrier(jnp.sum(old_weights, axis=-1)) + lax.optimization_barrier(jnp.sum(new_weights, axis=-1))
        old_rounded = lax.optimization_barrier(old_weights.astype(jnp.bfloat16)).astype(jnp.float32)
        new_rounded = lax.optimization_barrier(new_weights.astype(jnp.bfloat16)).astype(jnp.float32)
        mixture = jnp.einsum('qkht,thd->qkhd', old_rounded, cache_values) + jnp.einsum('qkht,thd->qkhd', new_rounded, own_values)
        return mixture / totals[..., None]
    attended = lax.map(one_request, jnp.arange(REQ, dtype=jnp.int32))
    attended = attended.reshape(tokens, 2, KVH * HD).astype(jnp.bfloat16)
    attended = lax.optimization_barrier(attended)
    chosen = jnp.take_along_axis(router_logits, routes, axis=1)
    gate_probs = jax.nn.softmax(chosen, axis=1)
    projected = jnp.einsum('nkh,ehd->nked', attended.astype(jnp.float32), w_output.astype(jnp.float32))
    mixing = jnp.where(selector, gate_probs[:, :, None], 0.0)
    output = lax.optimization_barrier(jnp.sum(mixing[..., None] * projected, axis=(1, 2)))
    kept_rows = step_of < accepted[request_of]
    attn_out = jnp.where(kept_rows[:, None], output, 0.0)
    new_keys = jnp.where(kept_rows[:, None], keys_rotated.reshape(tokens, KVH * HD), 0.0)
    new_values = jnp.where(kept_rows[:, None], values_raw.reshape(tokens, KVH * HD), 0.0)
    return (attn_out, new_keys, new_values)
```

```python
import math

import jax
import jax.numpy as jnp
from jax import lax
from jax.experimental import pallas as pl
from jax.experimental.pallas import tpu as pltpu
from jax.sharding import PartitionSpec as P

MESH = pl.DeviceIdType.MESH
THETA = 10000.0
NEGATIVE = -1e30
FLOOR = -1e29
F32 = jnp.float32
BF16 = jnp.bfloat16
HD = 128
E = 8
S = 16

def plane_hops(d):
    return min(d[0], 4 - d[0]) + min(d[1], 4 - d[1])


PLANE = sorted([(dx, dy) for dx in range(4) for dy in range(4)], key=plane_hops)
RING = sorted(range(S), key=lambda d: min(d, S - d))
REACH = S // 4
NEAR = RING[1 : 2 * REACH + 1]
HEAD_BLOCKS = (PLANE[0:4], PLANE[4:8], PLANE[8:12], PLANE[12:16])
RING_BLOCKS = (RING[0:5], RING[5:9], RING[9:13], RING[13:16])


def iota(shape, dim):
    return lax.broadcasted_iota(jnp.int32, shape, dim)


def dot_nt(a, b):
    return lax.dot_general(a, b, (((1,), (1,)), ((), ())), preferred_element_type=F32)


def dot_nn(a, b):
    return jnp.dot(a, b, preferred_element_type=F32)


def plane_peer(s, dx, dy):
    return (s // 4 + dx) % 4 * 4 + (s % 4 + dy) % 4


def take_all(ref, count, sem):
    part = ref.at[pl.ds(0, count)]
    pltpu.make_async_copy(part, part, sem).wait()


def pair_rows(a, b):
    a = a.reshape(S, 1, 8, HD)
    b = b.reshape(S, 1, 8, HD)
    return jnp.concatenate([a, b], axis=1).reshape(S, 16, HD)


def kernel(
    hid_ref,
    logits_hbm,
    routes_hbm,
    wq_ref,
    wkv_ref,
    wo_ref,
    kc_ref,
    vc_ref,
    len_hbm,
    table_hbm,
    home_hbm,
    acc_hbm,
    out_ref,
    nk_ref,
    nv_ref,
    hid_buf,
    wq_buf,
    wkv_buf,
    wo_buf,
    kbuf,
    vbuf,
    bias_buf,
    r_pair,
    g_pair,
    q_out,
    q_in,
    kv_out,
    kv_in,
    q_buf,
    p4s,
    p4r,
    att_buf,
    p6s,
    p6r,
    logits_ref,
    routes_ref,
    len_ref,
    table_ref,
    home_ref,
    acc_ref,
    local_sem,
    send_sem,
    recv_sem,
    q_sem,
    att_sem,
    w_send,
    w_recv,
    ready_sem,
):
    s = lax.axis_index("seq")
    t = lax.axis_index("tensor")
    z = t // 2
    c = t % 2
    other = 2 * z + 1 - c

    mine = s * 2 + c

    barrier = pltpu.get_barrier_semaphore()

    def greet(seq, tensor):
        pl.semaphore_signal(barrier, inc=1, device_id=(seq, tensor), device_id_type=MESH)

    for hops in range(REACH, 0, -1):
        for d in (hops, S - hops):
            greet(s, 2 * ((z + d) % S) + c)
        for dx, dy in PLANE:
            if plane_hops((dx, dy)) == hops:
                greet(plane_peer(s, dx, dy), t)
                greet(plane_peer(s, dx, dy), other)
    greet(s, other)

    loads = [
        pltpu.make_async_copy(hid_ref, hid_buf.at[mine], local_sem.at[0]),
        pltpu.make_async_copy(wq_ref, wq_buf.at[c], local_sem.at[1]),
        pltpu.make_async_copy(wkv_ref, wkv_buf.at[c], local_sem.at[2]),
        pltpu.make_async_copy(wo_ref, wo_buf.at[c], local_sem.at[3]),
        pltpu.make_async_copy(routes_hbm, routes_ref, local_sem.at[4]),
        pltpu.make_async_copy(logits_hbm, logits_ref, local_sem.at[5]),
        pltpu.make_async_copy(len_hbm, len_ref, local_sem.at[6]),
        pltpu.make_async_copy(home_hbm, home_ref, local_sem.at[7]),
        pltpu.make_async_copy(acc_hbm, acc_ref, local_sem.at[8]),
        pltpu.make_async_copy(table_hbm, table_ref, local_sem.at[9]),
        pltpu.make_async_copy(kc_ref, kbuf, local_sem.at[10]),
        pltpu.make_async_copy(vc_ref, vbuf, local_sem.at[11]),
    ]
    for load in loads:
        load.start()

    for load in loads[4:10]:
        load.wait()
    r_lane = routes_ref[...].astype(F32)
    logits = logits_ref[...]
    which = iota((E, 256), 0).astype(F32)
    c0 = jnp.sum(jnp.where(which == r_lane[0:1], logits, 0.0), axis=0, keepdims=True)
    c1 = jnp.sum(jnp.where(which == r_lane[1:2], logits, 0.0), axis=0, keepdims=True)
    cm = jnp.maximum(c0, c1)
    e0 = jnp.exp(c0 - cm)
    e1 = jnp.exp(c1 - cm)
    total = e0 + e1
    row8 = iota((8, 256), 0)
    packed = jnp.where(
        row8 == 0,
        r_lane[0:1],
        jnp.where(row8 == 1, r_lane[1:2], jnp.where(row8 == 2, e0 / total, e1 / total)),
    )
    cols = jnp.transpose(packed).reshape(S, 2, 8, 8)
    cols = jnp.where(c == 0, cols[:, 0], cols[:, 1]).reshape(S * 8, 8)
    wide = (S * 8, HD)
    r0 = jnp.broadcast_to(cols[:, 0:1], wide)
    r1 = jnp.broadcast_to(cols[:, 1:2], wide)
    g0 = jnp.broadcast_to(cols[:, 2:3], wide)
    g1 = jnp.broadcast_to(cols[:, 3:4], wide)

    r_pair[...] = pair_rows(r0, r1)
    g_pair[...] = pair_rows(g0, g1)

    row = iota((8, HD), 0)
    lane = iota((8, HD), 1)
    len0 = len_ref[2 * t]
    len1 = len_ref[2 * t + 1]
    pos = (jnp.where(row < 4, len0, len1) + row % 4).astype(F32)
    inverse = jnp.exp((lane % 64).astype(F32) * (-2.0 / HD * math.log(THETA)))
    angles = pos * inverse
    cosine = jnp.cos(angles)
    sine = jnp.sin(angles)
    sine = jnp.where(lane < HD // 2, -sine, sine)

    row_w = iota((16, 512), 0)
    lane_w = iota((16, 512), 1)
    slot_w = lane_w // 64
    limits = []
    for r, length in ((0, len0), (1, len1)):
        req = 2 * t + r
        off = (s - home_ref[req] + S) % S
        lim = jnp.zeros((16, 512), jnp.int32)
        for m in range(4):
            j = off + S * m
            left = jnp.minimum(jnp.maximum(length - 64 * j, 0), 64)
            lim = jnp.where(slot_w == table_ref[req, j], left, lim)
        limits.append(lim)
    lim = jnp.where((row_w // 4) % 2 == 0, limits[0], limits[1])
    bias_buf[...] = jnp.where(lane_w % 64 < lim, 0.0, NEGATIVE)

    loads[0].wait()
    pl.semaphore_wait(barrier, 31 + len(NEAR))

    trades = [
        pltpu.make_async_remote_copy(
            src_ref=src,
            dst_ref=dst.at[c],
            send_sem=w_send.at[n],
            recv_sem=w_recv.at[n],
            device_id=(s, other),
            device_id_type=MESH,
        )
        for n, (src, dst) in enumerate([(wq_ref, wq_buf), (wkv_ref, wkv_buf), (wo_ref, wo_buf)])
    ]

    def send_hidden(d, core):
        pltpu.make_async_remote_copy(
            src_ref=hid_buf.at[mine],
            dst_ref=hid_buf.at[mine],
            send_sem=send_sem.at[0],
            recv_sem=recv_sem.at[0],
            device_id=(plane_peer(s, d[0], d[1]), 2 * z + core),
            device_id_type=MESH,
        ).start()

    for d in PLANE[:0:-1]:
        send_hidden(d, c)
        send_hidden(d, 1 - c)
    for trade in trades:
        trade.start()
    send_hidden((0, 0), 1 - c)

    for d in (REACH, S - REACH):
        pl.semaphore_signal(
            ready_sem, inc=1, device_id=(s, 2 * ((z + d) % S) + c), device_id_type=MESH
        )

    loads[1].wait()
    loads[2].wait()
    trades[0].wait_recv()
    trades[1].wait_recv()
    pick_r = iota((HD, HD), 0)
    pick_c = iota((HD, HD), 1)
    pick = (pick_c == (pick_r % 64) * 2 + pick_r // 64).astype(F32).astype(BF16)
    kv_a = dot_nn(pick, wkv_buf[0]).astype(BF16)
    kv_b = dot_nn(pick, wkv_buf[1]).astype(BF16)
    w_k = jnp.concatenate([kv_a[:64], kv_b[:64]], axis=0)
    w_v = jnp.concatenate([kv_a[64:], kv_b[64:]], axis=0)

    take_all(hid_buf, 31, recv_sem.at[0])
    x = hid_buf[...].astype(F32).reshape(S, 2, 16, 64)
    x = jnp.where(c == 0, x[:, :, :8], x[:, :, 8:])
    lhs = jnp.concatenate([x[:, 0], x[:, 1]], axis=-1).reshape(S * 8, HD).astype(BF16)
    q0 = jnp.zeros(wide, F32)
    q1 = jnp.zeros(wide, F32)
    for e in range(E):
        w = jnp.concatenate([wq_buf[0, e], wq_buf[1, e]], axis=0)
        y = dot_nn(lhs, w)
        q0 = jnp.where(r0 == e, y, q0)
        q1 = jnp.where(r1 == e, y, q1)
    q_out[...] = pair_rows(q0, q1)

    pl.semaphore_wait(ready_sem, 2)

    def send_sums(src, dst, n):
        for d in RING[:0:-1]:
            peer = (z + d) % S
            pltpu.make_async_remote_copy(
                src_ref=src.at[peer],
                dst_ref=dst.at[z],
                send_sem=send_sem.at[n],
                recv_sem=recv_sem.at[n],
                device_id=(s, 2 * peer + c),
                device_id_type=MESH,
            ).start()
        dst[z] = src[z]

    send_sums(q_out, q_in, 1)
    key_part = dot_nn(lhs, w_k)
    value_part = dot_nn(lhs, w_v)
    kv_out[...] = pair_rows(key_part, value_part)

    take_all(q_in, S - 1, recv_sem.at[1])
    q_raw = jnp.sum(q_in[...], axis=0)
    cos2 = jnp.concatenate([cosine, cosine], axis=0)
    sin2 = jnp.concatenate([sine, sine], axis=0)
    queries = (q_raw * cos2 + pltpu.roll(q_raw, HD // 2, 1) * sin2).astype(BF16)
    q_buf[s] = queries

    for dx, dy in PLANE[:0:-1]:
        pltpu.make_async_remote_copy(
            src_ref=q_buf.at[s],
            dst_ref=q_buf.at[s],
            send_sem=send_sem.at[3],
            recv_sem=q_sem.at[PLANE.index((-dx % 4, -dy % 4))],
            device_id=(plane_peer(s, dx, dy), t),
            device_id_type=MESH,
        ).start()

    send_sums(kv_out, kv_in, 2)

    loads[10].wait()
    loads[11].wait()
    scaling = 1.0 / math.sqrt(HD)
    lane16 = iota((16, HD), 1)

    def send_partial(h):
        return pltpu.make_async_remote_copy(
            src_ref=p4s.at[h],
            dst_ref=p4r.at[s],
            send_sem=send_sem.at[4],
            recv_sem=recv_sem.at[4],
            device_id=(h, t),
            device_id_type=MESH,
        )

    for block in HEAD_BLOCKS:
        heads = [plane_peer(s, dx, dy) for dx, dy in block]
        spans = [pl.ds(pl.multiple_of(h * HD, HD), HD) for h in heads]
        for d, h in zip(block, heads):
            if d != (0, 0):
                n = PLANE.index(d)
                pltpu.make_async_copy(q_buf.at[h], q_buf.at[h], q_sem.at[n]).wait()
        bias = bias_buf[...]
        sc = [dot_nt(q_buf[h], kbuf[:, :, sp].reshape(512, HD)) for h, sp in zip(heads, spans)]
        sc = [x * scaling + bias for x in sc]
        tops = [jnp.maximum(jnp.max(x, axis=-1, keepdims=True), FLOOR) for x in sc]
        ws = [jnp.exp(x - top) for x, top in zip(sc, tops)]
        sums = [jnp.sum(w, axis=-1, keepdims=True) for w in ws]
        outs = [dot_nn(w.astype(BF16), vbuf[:, :, sp].reshape(512, HD)) for w, sp in zip(ws, spans)]
        for u, h in enumerate(heads):
            top, total = tops[u], sums[u]
            hi = top.astype(BF16).astype(F32)
            mid = (top - hi).astype(BF16).astype(F32)
            low = top - hi - mid
            s_hi = total.astype(BF16).astype(F32)
            s_low = total - s_hi
            stats = jnp.where(lane16 == 0, hi, 0.0)
            stats = jnp.where(lane16 == 1, mid, stats)
            stats = jnp.where(lane16 == 2, low, stats)
            stats = jnp.where(lane16 == 3, s_hi, stats)
            stats = jnp.where(lane16 == 4, s_low, stats)
            p4s[h, 0] = outs[u].astype(BF16)
            p4s[h, 1] = stats.astype(BF16)
        for d, h in zip(block, heads):
            if d == (0, 0):
                p4r[s] = p4s[s]
            else:
                send_partial(h).start()

    take_all(kv_in, S - 1, recv_sem.at[2])
    kv_sum = jnp.sum(kv_in[...], axis=0)
    k_raw = kv_sum[:8]
    v_raw = kv_sum[8:]
    k_rot = k_raw * cosine + pltpu.roll(k_raw, HD // 2, 1) * sine
    accept0 = acc_ref[2 * t]
    accept1 = acc_ref[2 * t + 1]
    kept = row % 4 < jnp.where(row < 4, accept0, accept1)
    nk_ref[...] = jnp.where(kept, k_rot, 0.0)
    nv_ref[...] = jnp.where(kept, v_raw, 0.0)
    zeros8 = jnp.zeros((8, HD), F32)
    k_fresh = jnp.concatenate([k_rot, zeros8], axis=0).astype(BF16)
    v_fresh = jnp.concatenate([v_raw, zeros8], axis=0).astype(BF16)
    f_tok = iota((16, 16), 0) % 8
    f_key = iota((16, 16), 1)
    causal = (f_key <= f_tok) & (f_key // 4 == f_tok // 4)
    f_scores = jnp.where(causal, dot_nt(queries, k_fresh) * scaling, NEGATIVE)
    f_top = jnp.max(f_scores, axis=-1, keepdims=True)
    f_w = jnp.exp(f_scores - f_top)
    f_sum = jnp.sum(f_w, axis=-1, keepdims=True)
    f_acc = dot_nn(f_w.astype(BF16), v_fresh)

    take_all(p4r, S - 1, recv_sem.at[4])
    er = iota((HD, 2 * HD), 0)
    ec = iota((HD, 2 * HD), 1)
    spread = jnp.where(ec < HD, er, er + 8)
    spread = ((spread < 3) | ((spread == 11) | (spread == 12))).astype(F32).astype(BF16)
    stat = dot_nn(p4r[:, 1].reshape(S * 16, HD), spread)
    tops = stat[:, :HD].reshape(S, 16, HD)
    sums = stat[:, HD:].reshape(S, 16, HD)
    top = jnp.maximum(jnp.max(tops, axis=0), f_top)
    factor = jnp.exp(tops - top[None])
    f_factor = jnp.exp(f_top - top)
    total = jnp.sum(factor * sums, axis=0) + f_factor * f_sum
    mixed = jnp.sum(factor * p4r[:, 0].astype(F32), axis=0) + f_factor * f_acc
    att_buf[z] = (mixed / total).astype(BF16)

    for d in RING[:0:-1]:
        pltpu.make_async_remote_copy(
            src_ref=att_buf.at[z],
            dst_ref=att_buf.at[z],
            send_sem=send_sem.at[5],
            recv_sem=att_sem.at[(S - d) % S],
            device_id=(s, 2 * ((z + d) % S) + c),
            device_id_type=MESH,
        ).start()
    loads[3].wait()
    trades[2].wait_recv()
    take_all(hid_buf, 31, send_sem.at[0])
    take_all(q_in, S - 1, send_sem.at[1])
    take_all(kv_in, S - 1, send_sem.at[2])
    take_all(q_buf, S - 1, send_sem.at[3])
    for trade in trades:
        trade.wait_send()

    def send_rows(to, core):
        return pltpu.make_async_remote_copy(
            src_ref=p6s.at[core, to],
            dst_ref=p6r.at[mine],
            send_sem=send_sem.at[6],
            recv_sem=recv_sem.at[6],
            device_id=(to, 2 * z + core),
            device_id_type=MESH,
        )

    for block in RING_BLOCKS:
        tos = [(z + d) % S for d in block]
        for d, to in zip(block, tos):
            if d != 0:
                pltpu.make_async_copy(att_buf.at[to], att_buf.at[to], att_sem.at[d]).wait()
        attended = jnp.concatenate([att_buf[to] for to in tos], axis=0)
        route = jnp.concatenate([r_pair[to] for to in tos], axis=0)
        gate = jnp.concatenate([g_pair[to] for to in tos], axis=0)
        chosen = jnp.zeros(route.shape, F32)
        for e in range(E):
            w = jnp.concatenate([wo_buf[0, e], wo_buf[1, e]], axis=0)
            chosen = jnp.where(route == e, dot_nt(attended, w), chosen)
        rows = (chosen * gate).reshape(len(block), 2, 8, HD)
        rows = rows[:, 0] + rows[:, 1]
        for u, to in enumerate(tos):
            p6s[0, to] = rows[u, :, :64]
            p6s[1, to] = rows[u, :, 64:]
            send_rows(to, 1 - c).start()

            @pl.when(to != s)
            def _():
                send_rows(to, c).start()

    p6r[mine] = p6s[c, s]
    take_all(p6r, 31, recv_sem.at[6])
    final = jnp.sum(p6r[...].reshape(S, 2, 8, 64), axis=0).reshape(16, 64)
    row_o = iota((16, 64), 0)
    step_lim = jnp.where(
        row_o < 8,
        jnp.where(row_o < 4, acc_ref[4 * s], acc_ref[4 * s + 1]),
        jnp.where(row_o < 12, acc_ref[4 * s + 2], acc_ref[4 * s + 3]),
    )
    out_ref[...] = jnp.where(row_o % 4 < step_lim, final, 0.0)

    take_all(p4r, S - 1, send_sem.at[4])
    take_all(att_buf, S - 1, send_sem.at[5])
    take_all(p6r, 31, send_sem.at[6])


def finish(attn_ref, keys_ref, values_ref, attn_out, keys_out, values_out, sem):
    copies = [
        pltpu.make_async_copy(attn_ref, attn_out, sem.at[0]),
        pltpu.make_async_copy(keys_ref, keys_out, sem.at[1]),
        pltpu.make_async_copy(values_ref, values_out, sem.at[2]),
    ]
    for copy in copies:
        copy.start()
    for copy in copies:
        copy.wait()


def per_device(
    hidden,
    router_logits,
    routes,
    w_query,
    w_keyval,
    w_output,
    k_cache,
    v_cache,
    lengths,
    page_table,
    home_device,
    accepted,
):
    vmem = pl.BlockSpec(memory_space=pltpu.VMEM)
    hbm = pl.BlockSpec(memory_space=pltpu.HBM)
    attn, keys, values = pl.pallas_call(
        kernel,
        out_shape=(
            jax.ShapeDtypeStruct((16, 64), F32),
            jax.ShapeDtypeStruct((8, HD), F32),
            jax.ShapeDtypeStruct((8, HD), F32),
        ),
        in_specs=[hbm] * 12,
        out_specs=(vmem, vmem, vmem),
        scratch_shapes=[
            pltpu.VMEM((32, 16, 64), BF16),
            pltpu.VMEM((2, E, 64, HD), BF16),
            pltpu.VMEM((2, HD, HD), BF16),
            pltpu.VMEM((2, E, 64, HD), BF16),
            pltpu.VMEM((8, 64, 2048), BF16),
            pltpu.VMEM((8, 64, 2048), BF16),
            pltpu.VMEM((16, 512), F32),
            pltpu.VMEM((S, 16, HD), F32),
            pltpu.VMEM((S, 16, HD), F32),
            pltpu.VMEM((S, 16, HD), F32),
            pltpu.VMEM((S, 16, HD), F32),
            pltpu.VMEM((S, 16, HD), F32),
            pltpu.VMEM((S, 16, HD), F32),
            pltpu.VMEM((S, 16, HD), BF16),
            pltpu.VMEM((S, 2, 16, HD), BF16),
            pltpu.VMEM((S, 2, 16, HD), BF16),
            pltpu.VMEM((S, 16, HD), BF16),
            pltpu.VMEM((2, S, 8, 64), F32),
            pltpu.VMEM((32, 8, 64), F32),
            pltpu.VMEM((E, 256), F32),
            pltpu.VMEM((2, 256), jnp.int32),
            pltpu.SMEM((64,), jnp.int32),
            pltpu.SMEM((64, 64), jnp.int32),
            pltpu.SMEM((64,), jnp.int32),
            pltpu.SMEM((64,), jnp.int32),
            pltpu.SemaphoreType.DMA((12,)),
            pltpu.SemaphoreType.DMA((7,)),
            pltpu.SemaphoreType.DMA((7,)),
            pltpu.SemaphoreType.DMA((S,)),
            pltpu.SemaphoreType.DMA((S,)),
            pltpu.SemaphoreType.DMA((3,)),
            pltpu.SemaphoreType.DMA((3,)),
            pltpu.SemaphoreType.REGULAR,
        ],
        compiler_params=pltpu.CompilerParams(
            collective_id=0, has_side_effects=True, vmem_limit_bytes=40 * 1024 * 1024
        ),
    )(
        *[
            pltpu.with_memory_space_constraint(a, pltpu.HBM)
            for a in (
                hidden,
                router_logits.T,
                routes.T,
                w_query,
                w_keyval.reshape(HD, HD),
                jnp.transpose(w_output, (0, 2, 1)),
                k_cache,
                v_cache,
                lengths,
                page_table,
                home_device,
                accepted,
            )
        ]
    )
    return pl.pallas_call(
        finish,
        out_shape=tuple(jax.ShapeDtypeStruct(a.shape, F32) for a in (attn, keys, values)),
        in_specs=[vmem] * 3,
        out_specs=(hbm,) * 3,
        scratch_shapes=[pltpu.SemaphoreType.DMA((3,))],
        compiler_params=pltpu.CompilerParams(vmem_limit_bytes=40 * 1024 * 1024),
    )(attn, keys, values)


def solution(mesh):
    in_specs = (
        P("seq", "tensor"),
        P(),
        P(),
        P(None, "tensor", "seq"),
        P("tensor", None, "seq"),
        P(None, "seq", "tensor"),
        P(("seq", "tensor"), None, None),
        P(("seq", "tensor"), None, None),
        P(),
        P(),
        P(),
        P(),
    )
    out_specs = (P("seq", "tensor"), P("tensor", "seq"), P("tensor", "seq"))
    return jax.shard_map(
        per_device, mesh=mesh, in_specs=in_specs, out_specs=out_specs, check_vma=False
    )
```
